128 devices in a mesh: row: 16 (over z, x), col: 8 (over y, core).
Axes of the slice: x: 4, y: 4, z: 4, core: 2. Of those that a mesh axis runs over, the one named last changes fastest.
Arguments:
- amplitudes: float32 [12288, 6144], P('row', 'col'), may hold values from -6 to 6
- integrals: float32 [6144, 6144], P('col', 'row'), may hold values from -0.125 to 0.125
- flags: int32 [64, 64], replicated, may hold values from 0 to 1, as said below
Outputs:
- ladder: float32 [12288, 6144], P('row', 'col')
The draws below stay inside these ranges and needn't reach their ends.
Inputs may be any that keep to these rules, and one draw needn't show every extreme that they name: `flags`: in each aligned block of 8 a-tiles by 4 d-tiles (tile rows k * 8 onward, tile columns m * 4 onward) at least 6 and at most 19 tile pairs are listed, and some block lists exactly 19.
All inputs are finite; a program needn't handle non-finite values.
Results may differ from the reference program's by a relative error of at most 0.00007.
Values sent between devices are 32-bit elements; how exact they have to be, the bound alone decides.
A program may use at most 192 MiB of HBM per device.

```python
import jax
import jax.numpy as jnp
from jax import lax

NT = 64
TILE = 96
NV = 6144
PAIRS = 12288
DR = 4
AC = 8
BLK = 32
CAP = 19


def draw_flags(key, part):
    rows_blocks = NT // AC
    cols_blocks = NT // DR
    key_count = jax.random.fold_in(key, 11)
    key_forced = jax.random.fold_in(key, 12)
    key_scores = jax.random.fold_in(key, 13)
    counts = jax.random.randint(key_count, (rows_blocks, cols_blocks), CAP // 3, CAP + 1)
    forced = jax.random.randint(key_forced, (), 0, rows_blocks * cols_blocks)
    block_ids = jnp.arange(rows_blocks * cols_blocks, dtype=jnp.int32).reshape(rows_blocks, cols_blocks)
    counts = jnp.where(block_ids == forced, CAP, counts)
    scores = jax.random.randint(key_scores, (rows_blocks, cols_blocks, BLK), 0, 2 ** 20) * BLK + jnp.arange(BLK, dtype=jnp.int32)
    rank_order = jnp.argsort(jnp.argsort(scores, axis=-1), axis=-1)
    listed = (rank_order < counts[..., None]).astype(jnp.int32)
    return listed.reshape(rows_blocks, cols_blocks, AC, DR).transpose(0, 2, 1, 3).reshape(NT, NT)


def levels(own_key, shape, cuts, low, largest):
    loudness = 1.0
    for dim, shards_of in cuts:
        draws = jax.random.uniform(jax.random.fold_in(jax.random.fold_in(own_key, 6), dim), (shards_of,), jnp.float32, low / len(cuts), largest / len(cuts))
        loudness = loudness * jnp.repeat(jnp.exp(draws), shape[dim] // shards_of).reshape((-1,) + (1,) * (len(shape) - 1 - dim))
    return loudness


def normal_values(stream_key, extent, width, reach, split=(), kind=jnp.bfloat16):
    entries = width * jax.random.normal(stream_key, extent, jnp.float32)
    if split:
        entries = entries * levels(stream_key, extent, split, -0.22, 0.18)
    return jnp.clip(entries, -reach, reach).astype(kind)


def setup_inputs(seed: int = 0) -> dict:
    arg_keys = jax.random.split(jax.random.key(seed), 4)
    return {
        "amplitudes": normal_values(arg_keys[0], (PAIRS, NV), 1.0, 6.0, ((0, 16), (1, 8)), jnp.float32),
        "integrals": normal_values(arg_keys[1], (NV, NV), (NV * 2 // 5) ** -0.5, 0.125, ((0, 8), (1, 16)), jnp.float32),
        "flags": draw_flags(jax.random.fold_in(arg_keys[3], 71), 0),
    }


def reference(amplitudes, integrals, flags):
    tile_mask = jnp.repeat(jnp.repeat(flags.astype(jnp.float32), TILE, axis=0), TILE, axis=1)
    screened = integrals * tile_mask
    return lax.dot_general(amplitudes, screened, (((1,), (1,)), ((), ())), precision=lax.Precision.HIGHEST, preferred_element_type=jnp.float32)
```

```python
import jax
import jax.numpy as jnp
from jax import lax
from jax.experimental import pallas as pl
from jax.experimental.pallas import tpu as pltpu
from jax.sharding import PartitionSpec as P

TILE = 96
CAP = 19
PIECE = 24
PIECES = 3 * CAP
MESH = pl.DeviceIdType.MESH
CHUNKS = 8
CHUNK = 96

FIRST, SECOND = (0, 29), (29, 28)
PASS_UP = {FIRST: (0, 14), SECOND: (29, 14)}
PASS_DOWN = {FIRST: (14, 15), SECOND: (43, 14)}


def lanes_of(rows):
    return lax.broadcasted_iota(jnp.int32, (rows, 128), 1)


def pack_kernel(flags_smem, flags_ref, x_ref, packed_ref, table_ref, turned):
    row, col = lax.axis_index("row"), lax.axis_index("col")
    own = flags_ref[pl.ds(pl.multiple_of(col * 8, 8), 8), :].astype(jnp.float32)
    d_from = lax.broadcasted_iota(jnp.int32, (64, 64), 0)
    d_to = lax.broadcasted_iota(jnp.int32, (64, 64), 1)
    earlier = ((d_from // 4 == d_to // 4) & (d_from < d_to)).astype(jnp.float32)
    i_to = lax.broadcasted_iota(jnp.int32, (8, 8), 0)
    i_from = lax.broadcasted_iota(jnp.int32, (8, 8), 1)
    above = (i_from < i_to).astype(jnp.float32)
    before = jnp.dot(own, earlier, preferred_element_type=jnp.float32)
    rank = jnp.dot(above, own, preferred_element_type=jnp.float32) + jnp.sum(before, axis=0, keepdims=True)
    table_ref[...] = (jnp.where(own > 0.5, rank, float(CAP)) * 3.0).astype(jnp.int32)

    packed_ref[...] = jnp.zeros_like(packed_ref)
    turned[...] = x_ref[...].T
    lane = lanes_of(TILE)
    count = jnp.int32(0)
    for j in range(4):
        for i in range(8):
            flag = flags_smem[col * 8 + i, row * 4 + j]

            @pl.when(flag != 0)
            def _():
                rows = slice(j * TILE, (j + 1) * TILE)
                first, offset = divmod(i * TILE, 128)
                tile = turned[rows, first * 128 : first * 128 + 128]
                if offset:
                    tile = pltpu.roll(tile, 128 - offset, 1)
                if offset > 32:
                    right = pltpu.roll(turned[rows, first * 128 + 128 : first * 128 + 256], 128 - offset, 1)
                    tile = jnp.where(lane < 128 - offset, tile, right)
                last = tile[3 * PIECE :]
                for q in range(3):
                    piece = tile[q * PIECE : (q + 1) * PIECE]
                    packed_ref[3 * count + q] = jnp.where(
                        lanes_of(PIECE) < TILE, piece, pltpu.roll(last, 96 - 32 * q, 1))

            count = count + flag


def split(value):
    high = value.astype(jnp.bfloat16)
    low = (value - high.astype(jnp.float32)).astype(jnp.bfloat16)
    return high, low


def main_kernel(table, amp_hbm, packed_hbm, out_ref, amp, b_high, b_low, *rest):
    blocks = {(dx, dz): rest[dx * 4 + dz] for dx in range(4) for dz in range(4)}
    send_sem, recv_sem, local_sem = rest[16:]
    row, col = lax.axis_index("row"), lax.axis_index("col")
    x, z = lax.rem(row, 4), lax.div(row, 4)
    k, y = lax.rem(col, 2), lax.div(col, 2)

    def at_x(d):
        return (z * 4 + lax.rem(x + d, 4), col)

    def at_z(d):
        return (lax.rem(z + d, 4) * 4 + x, col)

    def at_y(d):
        return (row, lax.rem(y + d, 4) * 2 + k)

    mate = (row, y * 2 + 1 - k)

    def column_of(d, core):
        return lax.rem(y + d, 4) * 2 + core

    barrier = pltpu.get_barrier_semaphore()
    for peer in (at_x(1), at_x(3), at_z(1), at_z(3), at_y(1), at_y(3), mate):
        pl.semaphore_signal(barrier, inc=1, device_id=peer, device_id_type=MESH)
    pl.semaphore_wait(barrier, 7)

    started = []

    def send(src, dst, device):
        n = len(started)
        copy = pltpu.make_async_remote_copy(
            src_ref=src, dst_ref=dst, send_sem=send_sem.at[n], recv_sem=recv_sem.at[n],
            device_id=device, device_id_type=MESH,
        )
        copy.start()
        started.append(copy)
        return copy

    def rows_of(q):
        return pl.ds(q * CHUNK, CHUNK)

    up, down, pass_up, pass_down, shared = {}, {}, {}, {}, {}
    up_order, down_order = (0, 1, 2, 3, 4, 5, 6, 7), (4, 5, 6, 7, 0, 1, 2, 3)

    def send_own(n):
        q = up_order[n]
        up[q] = send(amp_hbm.at[rows_of(q)], amp.at[col, rows_of(q)], at_y(1))
        q = down_order[n]
        down[q] = send(amp_hbm.at[rows_of(q)], amp.at[col, rows_of(q)], at_y(3))

    def part(ref, span):
        return ref.at[pl.ds(span[0], span[1])]

    ring = {}

    def key_of(half, phase, other, d):
        along_x = (half is FIRST) == (phase == 1)
        return (d, other) if along_x else (other, d)

    def peer_of(half, phase, d):
        return at_x(d) if (half is FIRST) == (phase == 1) else at_z(d)

    def ring_send(half, phase, other):
        own = key_of(half, phase, other, 0)
        src = packed_hbm if own == (0, 0) else blocks[own]
        ring[half, phase, other, "up"] = send(
            part(src, half), part(blocks[key_of(half, phase, other, 3)], half), peer_of(half, phase, 1))
        ring[half, phase, other, "down"] = send(
            part(src, half), part(blocks[key_of(half, phase, other, 1)], half), peer_of(half, phase, 3))

    def ring_pass(half, phase, other):
        ring[half, phase, other, "up"].wait_recv()
        far = blocks[key_of(half, phase, other, 2)]
        span = PASS_UP[half]
        ring[half, phase, other, "pass_up"] = send(
            part(blocks[key_of(half, phase, other, 3)], span), part(far, span), peer_of(half, phase, 1))
        ring[half, phase, other, "down"].wait_recv()
        span = PASS_DOWN[half]
        ring[half, phase, other, "pass_down"] = send(
            part(blocks[key_of(half, phase, other, 1)], span), part(far, span), peer_of(half, phase, 3))

    def ring_last(half, phase, other):
        ring[half, phase, other, "pass_up"].wait_recv()
        ring[half, phase, other, "pass_down"].wait_recv()

    halves = (FIRST, SECOND)

    send_own(0)
    for half in halves:
        ring_send(half, 1, 0)
    for half in halves:
        ring_send(half, 2, 0)
    own_amp = pltpu.make_async_copy(amp_hbm, amp.at[col], local_sem.at[0])
    own_amp.start()
    own_block = pltpu.make_async_copy(packed_hbm, blocks[0, 0].at[pl.ds(0, PIECES)], local_sem.at[1])
    own_block.start()
    for n in range(1, CHUNKS):
        send_own(n)
    shared["own"] = send(amp_hbm, amp.at[col], mate)

    def share(key, column, q):
        shared[key] = send(amp.at[column, rows_of(q)], amp.at[column, rows_of(q)], mate)

    def y_step(n):
        below, above = column_of(3, k), column_of(1, k)
        q = up_order[n]
        up[q].wait_recv()
        if n < 4:
            pass_up[q] = send(amp.at[below, rows_of(q)], amp.at[below, rows_of(q)], at_y(1))
        share(("below", q), below, q)
        q = down_order[n]
        down[q].wait_recv()
        if n < 4:
            pass_down[q] = send(amp.at[above, rows_of(q)], amp.at[above, rows_of(q)], at_y(3))
        share(("above", q), above, q)

    def y_last(n):
        far = column_of(2, k)
        q = up_order[n]
        pass_up[q].wait_recv()
        share(("far", q), far, q)
        q = down_order[n]
        pass_down[q].wait_recv()
        share(("far", q), far, q)

    lane24, lane96 = lanes_of(PIECE), lanes_of(TILE)

    def unpack(dx, dz):
        block = blocks[dx, dz]
        xs, zs = lax.rem(x + dx, 4), lax.rem(z + dz, 4)
        source = zs * 4 + xs
        column = lax.div(source, 2)
        base = lax.rem(source, 2) * 384

        @pl.loop(0, 4)
        def _(j):
            target = pl.ds(pl.multiple_of(base + j * TILE, 32), TILE)
            for group in range(2):
                tiles = []
                for i in range(4):
                    start = table[group * 4 + i, source * 4 + j]
                    pieces = [block[start + q] for q in range(3)]
                    turned = [pltpu.roll(pieces[q], 32 + 32 * q, 1) for q in range(3)]
                    last = jnp.where(lane24 < 32, turned[0], jnp.where(lane24 < 64, turned[1], turned[2]))
                    tile = jnp.concatenate(pieces + [last], axis=0)
                    if i:
                        tile = pltpu.roll(tile, 128 - 32 * i, 1)
                    tiles.append(tile)
                for i in range(3):
                    high, low = split(jnp.where(lane96 < 96 - 32 * i, tiles[i], tiles[i + 1]))
                    lanes = pl.ds((group * 3 + i) * 128, 128)
                    b_high[column, target, lanes] = high
                    b_low[column, target, lanes] = low

    def product(column, rows):
        a_high, a_low = split(amp[column, rows, :])
        high, low = b_high[column], b_low[column]
        total = jnp.dot(a_high, high, preferred_element_type=jnp.float32)
        total += jnp.dot(a_high, low, preferred_element_type=jnp.float32)
        total += jnp.dot(a_low, high, preferred_element_type=jnp.float32)
        return total

    def multiply(columns, first=False):
        for n, column in enumerate(columns):

            @pl.loop(0, 3)
            def _(m):
                rows = pl.ds(pl.multiple_of(m * 256, 256), 256)
                value = product(column, rows)
                if first and n == 0:
                    out_ref[rows, :] = value
                else:
                    out_ref[rows, :] += value

    for block in blocks.values():
        block[PIECES:] = jnp.zeros((3, PIECE, 128), jnp.float32)

    own_block.wait()
    unpack(0, 0)
    y_step(0)
    for half in halves:
        ring_pass(half, 1, 0)
    for other in (3, 1):
        for half in halves:
            ring_send(half, 2, other)
    y_step(1)
    for half in halves:
        ring_pass(half, 2, 0)
    for key in ((0, 3), (0, 1), (3, 0), (1, 0)):
        unpack(*key)
    y_step(2)
    for half in halves:
        ring_last(half, 1, 0)
    for half in halves:
        ring_send(half, 2, 2)
    y_step(3)
    for half in halves:
        ring_pass(half, 2, 3)
    unpack(3, 3)
    y_step(4)
    for half in halves:
        ring_pass(half, 2, 1)
    for key in ((3, 1), (1, 3), (1, 1)):
        unpack(*key)
    y_step(5)
    for half in halves:
        ring_pass(half, 2, 2)
    y_step(6)
    for half in halves:
        ring_last(half, 2, 0)
    unpack(2, 0)
    unpack(0, 2)
    own_amp.wait()
    shared["own"].wait_recv()
    for half in halves:
        ring_last(half, 2, 3)
    unpack(2, 3)
    unpack(3, 2)
    y_step(7)
    for half in halves:
        ring_last(half, 2, 1)
    unpack(2, 1)
    unpack(1, 2)
    for half in halves:
        ring_last(half, 2, 2)
    unpack(2, 2)

    multiply((col, mate[1]), first=True)
    y_last(0)
    for q in range(CHUNKS):
        shared["below", q].wait_recv()
    multiply((column_of(3, k), column_of(3, 1 - k)))
    y_last(1)
    for q in range(CHUNKS):
        shared["above", q].wait_recv()
    multiply((column_of(1, k), column_of(1, 1 - k)))
    y_last(2)

    def finish(n):
        for q in (up_order[n], down_order[n]):
            shared["far", q].wait_recv()
            rows = rows_of(q)
            out_ref[rows, :] += product(column_of(2, k), rows) + product(column_of(2, 1 - k), rows)

    finish(0)
    finish(1)
    finish(2)
    y_last(3)
    finish(3)
    for copy in started:
        copy.wait_send()


COPIES = 2 * CHUNKS + 1 + CHUNKS + 3 * CHUNKS + 40


def body(amplitudes, integrals, flags):
    packed, table = pl.pallas_call(
        pack_kernel,
        out_shape=(
            jax.ShapeDtypeStruct((PIECES, PIECE, 128), jnp.float32),
            jax.ShapeDtypeStruct((8, 64), jnp.int32),
        ),
        in_specs=[
            pl.BlockSpec(memory_space=pltpu.SMEM),
            pl.BlockSpec(memory_space=pltpu.VMEM),
            pl.BlockSpec(memory_space=pltpu.VMEM),
        ],
        out_specs=(pl.BlockSpec(memory_space=pltpu.VMEM), pl.BlockSpec(memory_space=pltpu.VMEM)),
        scratch_shapes=[pltpu.VMEM((384, 768), jnp.float32)],
        name="pack",
    )(flags, flags, integrals)
    return pl.pallas_call(
        main_kernel,
        out_shape=jax.ShapeDtypeStruct((768, 768), jnp.float32),
        in_specs=[
            pl.BlockSpec(memory_space=pltpu.SMEM),
            pl.BlockSpec(memory_space=pl.ANY),
            pl.BlockSpec(memory_space=pl.ANY),
        ],
        out_specs=pl.BlockSpec(memory_space=pltpu.VMEM),
        scratch_shapes=[
            pltpu.VMEM((8, 768, 768), jnp.float32),
            pltpu.VMEM((8, 768, 768), jnp.bfloat16),
            pltpu.VMEM((8, 768, 768), jnp.bfloat16),
        ]
        + [pltpu.VMEM((PIECES + 3, PIECE, 128), jnp.float32)] * 16
        + [
            pltpu.SemaphoreType.DMA((COPIES,)),
            pltpu.SemaphoreType.DMA((COPIES,)),
            pltpu.SemaphoreType.DMA((2,)),
        ],
        compiler_params=pltpu.CompilerParams(
            collective_id=0, has_side_effects=True, vmem_limit_bytes=66_000_000
        ),
        name="ladder",
    )(table, amplitudes, packed)


def solution(mesh):
    return jax.shard_map(
        body,
        mesh=mesh,
        in_specs=(P("row", "col"), P("col", "row"), P()),
        out_specs=P("row", "col"),
        check_vma=False,
    )
```

```python
import jax
import jax.numpy as jnp
from jax import lax
from jax.experimental import pallas as pl
from jax.experimental.pallas import tpu as pltpu
from jax.sharding import PartitionSpec as P

TILE = 96
CAP = 19
PIECE = 24
PIECES = 3 * CAP
MESH = pl.DeviceIdType.MESH
CHUNKS = 8
CHUNK = 96

FIRST, SECOND = (0, 29), (29, 28)
PASS_UP = {FIRST: (0, 14), SECOND: (29, 14)}
PASS_DOWN = {FIRST: (14, 15), SECOND: (43, 14)}


def lanes_of(rows):
    return lax.broadcasted_iota(jnp.int32, (rows, 128), 1)


def pack_kernel(flags_smem, flags_ref, x_ref, packed_ref, table_ref, turned):
    row, col = lax.axis_index("row"), lax.axis_index("col")
    own = flags_ref[pl.ds(pl.multiple_of(col * 8, 8), 8), :].astype(jnp.float32)
    d_from = lax.broadcasted_iota(jnp.int32, (64, 64), 0)
    d_to = lax.broadcasted_iota(jnp.int32, (64, 64), 1)
    earlier = ((d_from // 4 == d_to // 4) & (d_from < d_to)).astype(jnp.float32)
    i_to = lax.broadcasted_iota(jnp.int32, (8, 8), 0)
    i_from = lax.broadcasted_iota(jnp.int32, (8, 8), 1)
    above = (i_from < i_to).astype(jnp.float32)
    before = jnp.dot(own, earlier, preferred_element_type=jnp.float32)
    rank = jnp.dot(above, own, preferred_element_type=jnp.float32) + jnp.sum(before, axis=0, keepdims=True)
    table_ref[...] = (jnp.where(own > 0.5, rank, float(CAP)) * 3.0).astype(jnp.int32)

    packed_ref[...] = jnp.zeros_like(packed_ref)
    turned[...] = x_ref[...].T
    lane = lanes_of(TILE)
    count = jnp.int32(0)
    for j in range(4):
        for i in range(8):
            flag = flags_smem[col * 8 + i, row * 4 + j]

            @pl.when(flag != 0)
            def _():
                rows = slice(j * TILE, (j + 1) * TILE)
                first, offset = divmod(i * TILE, 128)
                tile = turned[rows, first * 128 : first * 128 + 128]
                if offset:
                    tile = pltpu.roll(tile, 128 - offset, 1)
                if offset > 32:
                    right = pltpu.roll(turned[rows, first * 128 + 128 : first * 128 + 256], 128 - offset, 1)
                    tile = jnp.where(lane < 128 - offset, tile, right)
                last = tile[3 * PIECE :]
                for q in range(3):
                    piece = tile[q * PIECE : (q + 1) * PIECE]
                    packed_ref[3 * count + q] = jnp.where(
                        lanes_of(PIECE) < TILE, piece, pltpu.roll(last, 96 - 32 * q, 1))

            count = count + flag


def split(value):
    high = value.astype(jnp.bfloat16)
    low = (value - high.astype(jnp.float32)).astype(jnp.bfloat16)
    return high, low


def main_kernel(table, amp_hbm, packed_hbm, out_ref, amp, b_high, b_low, *rest):
    blocks = {(dx, dz): rest[dx * 4 + dz] for dx in range(4) for dz in range(4)}
    send_sem, recv_sem, local_sem = rest[16:]
    row, col = lax.axis_index("row"), lax.axis_index("col")
    x, z = lax.rem(row, 4), lax.div(row, 4)
    k, y = lax.rem(col, 2), lax.div(col, 2)

    def at_x(d):
        return (z * 4 + lax.rem(x + d, 4), col)

    def at_z(d):
        return (lax.rem(z + d, 4) * 4 + x, col)

    def at_y(d):
        return (row, lax.rem(y + d, 4) * 2 + k)

    mate = (row, y * 2 + 1 - k)

    def column_of(d, core):
        return lax.rem(y + d, 4) * 2 + core

    barrier = pltpu.get_barrier_semaphore()
    for peer in (at_x(1), at_x(3), at_z(1), at_z(3), at_y(1), at_y(3), mate):
        pl.semaphore_signal(barrier, inc=1, device_id=peer, device_id_type=MESH)
    pl.semaphore_wait(barrier, 7)

    started = []

    def send(src, dst, device):
        n = len(started)
        copy = pltpu.make_async_remote_copy(
            src_ref=src, dst_ref=dst, send_sem=send_sem.at[n], recv_sem=recv_sem.at[n],
            device_id=device, device_id_type=MESH,
        )
        copy.start()
        started.append(copy)
        return copy

    def rows_of(q):
        return pl.ds(q * CHUNK, CHUNK)

    up, down, pass_up, pass_down, shared = {}, {}, {}, {}, {}
    up_order, down_order = (0, 1, 2, 3, 4, 5, 6, 7), (4, 5, 6, 7, 0, 1, 2, 3)

    def send_own(n):
        q = up_order[n]
        up[q] = send(amp_hbm.at[rows_of(q)], amp.at[col, rows_of(q)], at_y(1))
        q = down_order[n]
        down[q] = send(amp_hbm.at[rows_of(q)], amp.at[col, rows_of(q)], at_y(3))

    def part(ref, span):
        return ref.at[pl.ds(span[0], span[1])]

    ring = {}

    def key_of(half, phase, other, d):
        along_x = (half is FIRST) == (phase == 1)
        return (d, other) if along_x else (other, d)

    def peer_of(half, phase, d):
        return at_x(d) if (half is FIRST) == (phase == 1) else at_z(d)

    def ring_send(half, phase, other):
        own = key_of(half, phase, other, 0)
        src = packed_hbm if own == (0, 0) else blocks[own]
        ring[half, phase, other, "up"] = send(
            part(src, half), part(blocks[key_of(half, phase, other, 3)], half), peer_of(half, phase, 1))
        ring[half, phase, other, "down"] = send(
            part(src, half), part(blocks[key_of(half, phase, other, 1)], half), peer_of(half, phase, 3))

    def ring_pass(half, phase, other):
        ring[half, phase, other, "up"].wait_recv()
        far = blocks[key_of(half, phase, other, 2)]
        span = PASS_UP[half]
        ring[half, phase, other, "pass_up"] = send(
            part(blocks[key_of(half, phase, other, 3)], span), part(far, span), peer_of(half, phase, 1))
        ring[half, phase, other, "down"].wait_recv()
        span = PASS_DOWN[half]
        ring[half, phase, other, "pass_down"] = send(
            part(blocks[key_of(half, phase, other, 1)], span), part(far, span), peer_of(half, phase, 3))

    def ring_last(half, phase, other):
        ring[half, phase, other, "pass_up"].wait_recv()
        ring[half, phase, other, "pass_down"].wait_recv()

    halves = (FIRST, SECOND)

    send_own(0)
    for half in halves:
        ring_send(half, 1, 0)
    for half in halves:
        ring_send(half, 2, 0)
    own_amp = pltpu.make_async_copy(amp_hbm, amp.at[col], local_sem.at[0])
    own_amp.start()
    own_block = pltpu.make_async_copy(packed_hbm, blocks[0, 0].at[pl.ds(0, PIECES)], local_sem.at[1])
    own_block.start()
    for n in range(1, CHUNKS):
        send_own(n)
    shared["own"] = send(amp_hbm, amp.at[col], mate)

    def share(key, column, q):
        shared[key] = send(amp.at[column, rows_of(q)], amp.at[column, rows_of(q)], mate)

    def y_step(n):
        below, above = column_of(3, k), column_of(1, k)
        q = up_order[n]
        up[q].wait_recv()
        if n < 4:
            pass_up[q] = send(amp.at[below, rows_of(q)], amp.at[below, rows_of(q)], at_y(1))
        share(("below", q), below, q)
        q = down_order[n]
        down[q].wait_recv()
        if n < 4:
            pass_down[q] = send(amp.at[above, rows_of(q)], amp.at[above, rows_of(q)], at_y(3))
        share(("above", q), above, q)

    def y_last(n):
        far = column_of(2, k)
        q = up_order[n]
        pass_up[q].wait_recv()
        share(("far", q), far, q)
        q = down_order[n]
        pass_down[q].wait_recv()
        share(("far", q), far, q)

    lane24, lane96 = lanes_of(PIECE), lanes_of(TILE)

    def unpack(dx, dz):
        block = blocks[dx, dz]
        xs, zs = lax.rem(x + dx, 4), lax.rem(z + dz, 4)
        source = zs * 4 + xs
        column = lax.div(source, 2)
        base = lax.rem(source, 2) * 384

        @pl.loop(0, 4)
        def _(j):
            target = pl.ds(pl.multiple_of(base + j * TILE, 32), TILE)
            for group in range(2):
                tiles = []
                for i in range(4):
                    start = table[group * 4 + i, source * 4 + j]
                    pieces = [block[start + q] for q in range(3)]
                    turned = [pltpu.roll(pieces[q], 32 + 32 * q, 1) for q in range(3)]
                    last = jnp.where(lane24 < 32, turned[0], jnp.where(lane24 < 64, turned[1], turned[2]))
                    tile = jnp.concatenate(pieces + [last], axis=0)
                    if i:
                        tile = pltpu.roll(tile, 128 - 32 * i, 1)
                    tiles.append(tile)
                for i in range(3):
                    high, low = split(jnp.where(lane96 < 96 - 32 * i, tiles[i], tiles[i + 1]))
                    lanes = pl.ds((group * 3 + i) * 128, 128)
                    b_high[column, target, lanes] = high
                    b_low[column, target, lanes] = low

    def product(column, left):
        a_high, a_low = split(left)
        high, low = b_high[column], b_low[column]
        return jnp.dot(
            jnp.concatenate([a_high, a_high, a_low], axis=1),
            jnp.concatenate([high, low, high], axis=0),
            preferred_element_type=jnp.float32,
        )

    near = lax.div(x, 2)

    def multiply(dz, core, half, wanted):
        zs = lax.rem(z + dz, 4)
        dy = lax.rem(zs + 4 - y, 4)
        first = (dy == 0) | ((dy == 3) & (half == 0)) | ((dy == 1) & (half == 1))

        @pl.when(wanted(dy, first))
        def _():
            rows = pl.ds(pl.multiple_of(half * 384, 384), 384)
            column = zs * 2 + core
            out_ref[rows, :] += product(column, amp[column, rows, :])

    for block in blocks.values():
        block[PIECES:] = jnp.zeros((3, PIECE, 128), jnp.float32)
    out_ref[...] = jnp.zeros_like(out_ref)

    own_block.wait()
    unpack(0, 0)
    y_step(0)
    for half in halves:
        ring_pass(half, 1, 0)
    for other in (3, 1):
        for half in halves:
            ring_send(half, 2, other)
    y_step(1)
    for half in halves:
        ring_pass(half, 2, 0)
    for key in ((0, 3), (0, 1), (3, 0), (1, 0)):
        unpack(*key)
    y_step(2)
    for half in halves:
        ring_last(half, 1, 0)
    for half in halves:
        ring_send(half, 2, 2)
    y_step(3)
    for half in halves:
        ring_pass(half, 2, 3)
    unpack(3, 3)
    y_step(4)
    for half in halves:
        ring_pass(half, 2, 1)
    for key in ((3, 1), (1, 3), (1, 1)):
        unpack(*key)
    own_amp.wait()
    shared["own"].wait_recv()
    for q in range(4):
        shared["below", q].wait_recv()
        shared["above", q + 4].wait_recv()

    @pl.loop(0, 6)
    def _(n):
        multiply(lax.rem(3 + lax.div(n, 2), 4), near, lax.rem(n, 2), lambda dy, first: first)

    y_step(5)
    for half in halves:
        ring_pass(half, 2, 2)
    y_step(6)
    for half in halves:
        ring_last(half, 2, 0)
    unpack(2, 0)
    unpack(0, 2)
    for half in halves:
        ring_last(half, 2, 3)
    unpack(2, 3)
    unpack(3, 2)
    y_step(7)
    for half in halves:
        ring_last(half, 2, 1)
    unpack(2, 1)
    unpack(1, 2)
    for q in range(4):
        shared["below", q + 4].wait_recv()
        shared["above", q].wait_recv()

    @pl.loop(0, 14)
    def _(n):
        entry = lax.div(n, 2)
        done = entry < 3
        core = jnp.where(entry < 4, near, 1 - near)
        multiply(
            lax.rem(3 + entry, 4), core, lax.rem(n, 2),
            lambda dy, first: (dy != 2) & jnp.logical_not(done & first))

    y_last(0)
    for half in halves:
        ring_last(half, 2, 2)
    unpack(2, 2)

    @pl.loop(0, 2)
    def _(n):
        multiply(jnp.int32(2), 1 - near, n, lambda dy, first: dy != 2)

    def finish(n, column):
        rows = [rows_of(q) for q in (up_order[n], down_order[n])]
        value = product(column, jnp.concatenate([amp[column, r, :] for r in rows], axis=0))
        out_ref[rows[0], :] += value[:CHUNK]
        out_ref[rows[1], :] += value[CHUNK:]

    def finish_shared(n):
        for q in (up_order[n], down_order[n]):
            shared["far", q].wait_recv()
        finish(n, column_of(2, 1 - k))

    y_last(1)
    finish(0, column_of(2, k))
    finish_shared(0)
    finish(1, column_of(2, k))
    y_last(2)
    finish_shared(1)
    finish(2, column_of(2, k))
    y_last(3)
    finish_shared(2)
    finish(3, column_of(2, k))
    finish_shared(3)
    for copy in started:
        copy.wait_send()


COPIES = 2 * CHUNKS + 1 + CHUNKS + 3 * CHUNKS + 40


def body(amplitudes, integrals, flags):
    packed, table = pl.pallas_call(
        pack_kernel,
        out_shape=(
            jax.ShapeDtypeStruct((PIECES, PIECE, 128), jnp.float32),
            jax.ShapeDtypeStruct((8, 64), jnp.int32),
        ),
        in_specs=[
            pl.BlockSpec(memory_space=pltpu.SMEM),
            pl.BlockSpec(memory_space=pltpu.VMEM),
            pl.BlockSpec(memory_space=pltpu.VMEM),
        ],
        out_specs=(pl.BlockSpec(memory_space=pltpu.VMEM), pl.BlockSpec(memory_space=pltpu.VMEM)),
        scratch_shapes=[pltpu.VMEM((384, 768), jnp.float32)],
        name="pack",
    )(flags, flags, integrals)
    return pl.pallas_call(
        main_kernel,
        out_shape=jax.ShapeDtypeStruct((768, 768), jnp.float32),
        in_specs=[
            pl.BlockSpec(memory_space=pltpu.SMEM),
            pl.BlockSpec(memory_space=pl.ANY),
            pl.BlockSpec(memory_space=pl.ANY),
        ],
        out_specs=pl.BlockSpec(memory_space=pltpu.VMEM),
        scratch_shapes=[
            pltpu.VMEM((8, 768, 768), jnp.float32),
            pltpu.VMEM((8, 768, 768), jnp.bfloat16),
            pltpu.VMEM((8, 768, 768), jnp.bfloat16),
        ]
        + [pltpu.VMEM((PIECES + 3, PIECE, 128), jnp.float32)] * 16
        + [
            pltpu.SemaphoreType.DMA((COPIES,)),
            pltpu.SemaphoreType.DMA((COPIES,)),
            pltpu.SemaphoreType.DMA((2,)),
        ],
        compiler_params=pltpu.CompilerParams(
            collective_id=0, has_side_effects=True, vmem_limit_bytes=66_000_000
        ),
        name="ladder",
    )(table, amplitudes, packed)


def solution(mesh):
    return jax.shard_map(
        body,
        mesh=mesh,
        in_specs=(P("row", "col"), P("col", "row"), P()),
        out_specs=P("row", "col"),
        check_vma=False,
    )
```

```python
import jax
import jax.numpy as jnp
from jax import lax
from jax.experimental import pallas as pl
from jax.experimental.pallas import tpu as pltpu
from jax.sharding import PartitionSpec as P

TILE = 96
CAP = 19
PIECE = 24
PIECES = 3 * CAP
MESH = pl.DeviceIdType.MESH
CHUNKS = 8
CHUNK = 96

FIRST, SECOND = (0, 29), (29, 28)
PASS_UP = {FIRST: (0, 14), SECOND: (29, 14)}
PASS_DOWN = {FIRST: (14, 15), SECOND: (43, 14)}


def lanes_of(rows):
    return lax.broadcasted_iota(jnp.int32, (rows, 128), 1)


def split(value):
    high = value.astype(jnp.bfloat16)
    low = (value - high.astype(jnp.float32)).astype(jnp.bfloat16)
    return high, low


def main_kernel(flags, amp_hbm, x_hbm, out_ref, amp, b_high, b_low, x_ref, turned, tiles, table, *rest):
    blocks = {(dx, dz): rest[dx * 4 + dz] for dx in range(4) for dz in range(4)}
    send_sem, recv_sem, local_sem = rest[16:]
    row, col = lax.axis_index("row"), lax.axis_index("col")
    x, z = lax.rem(row, 4), lax.div(row, 4)
    k, y = lax.rem(col, 2), lax.div(col, 2)

    def at_x(d):
        return (z * 4 + lax.rem(x + d, 4), col)

    def at_z(d):
        return (lax.rem(z + d, 4) * 4 + x, col)

    def at_y(d):
        return (row, lax.rem(y + d, 4) * 2 + k)

    mate = (row, y * 2 + 1 - k)

    def column_of(d, core):
        return lax.rem(y + d, 4) * 2 + core

    own_x = pltpu.make_async_copy(x_hbm, x_ref, local_sem.at[1])
    own_x.start()
    own_amp = pltpu.make_async_copy(amp_hbm, amp.at[col], local_sem.at[0])
    own_amp.start()

    barrier = pltpu.get_barrier_semaphore()
    for peer in (at_x(1), at_x(3), at_z(1), at_z(3), at_y(1), at_y(3), mate):
        pl.semaphore_signal(barrier, inc=1, device_id=peer, device_id_type=MESH)
    pl.semaphore_wait(barrier, 7)

    started = []

    def send(src, dst, device):
        n = len(started)
        copy = pltpu.make_async_remote_copy(
            src_ref=src, dst_ref=dst, send_sem=send_sem.at[n], recv_sem=recv_sem.at[n],
            device_id=device, device_id_type=MESH,
        )
        copy.start()
        started.append(copy)
        return copy

    def rows_of(q):
        return pl.ds(q * CHUNK, CHUNK)

    up, down, pass_up, pass_down, shared = {}, {}, {}, {}, {}
    up_order, down_order = (0, 1, 2, 3, 4, 5, 6, 7), (4, 5, 6, 7, 0, 1, 2, 3)

    def send_own(n):
        q = up_order[n]
        up[q] = send(amp_hbm.at[rows_of(q)], amp.at[col, rows_of(q)], at_y(1))
        q = down_order[n]
        down[q] = send(amp_hbm.at[rows_of(q)], amp.at[col, rows_of(q)], at_y(3))

    def part(ref, span):
        return ref.at[pl.ds(span[0], span[1])]

    ring = {}

    def key_of(half, phase, other, d):
        along_x = (half is FIRST) == (phase == 1)
        return (d, other) if along_x else (other, d)

    def peer_of(half, phase, d):
        return at_x(d) if (half is FIRST) == (phase == 1) else at_z(d)

    def ring_send(half, phase, other):
        src = blocks[key_of(half, phase, other, 0)]
        ring[half, phase, other, "up"] = send(
            part(src, half), part(blocks[key_of(half, phase, other, 3)], half), peer_of(half, phase, 1))
        ring[half, phase, other, "down"] = send(
            part(src, half), part(blocks[key_of(half, phase, other, 1)], half), peer_of(half, phase, 3))

    def ring_pass(half, phase, other):
        ring[half, phase, other, "up"].wait_recv()
        far = blocks[key_of(half, phase, other, 2)]
        span = PASS_UP[half]
        ring[half, phase, other, "pass_up"] = send(
            part(blocks[key_of(half, phase, other, 3)], span), part(far, span), peer_of(half, phase, 1))
        ring[half, phase, other, "down"].wait_recv()
        span = PASS_DOWN[half]
        ring[half, phase, other, "pass_down"] = send(
            part(blocks[key_of(half, phase, other, 1)], span), part(far, span), peer_of(half, phase, 3))

    def ring_last(half, phase, other):
        ring[half, phase, other, "pass_up"].wait_recv()
        ring[half, phase, other, "pass_down"].wait_recv()

    halves = (FIRST, SECOND)

    for n in range(CHUNKS):
        send_own(n)
    shared["own"] = send(amp_hbm, amp.at[col], mate)

    def share(key, column, q):
        shared[key] = send(amp.at[column, rows_of(q)], amp.at[column, rows_of(q)], mate)

    def y_step(n):
        below, above = column_of(3, k), column_of(1, k)
        q = up_order[n]
        up[q].wait_recv()
        if n < 4:
            pass_up[q] = send(amp.at[below, rows_of(q)], amp.at[below, rows_of(q)], at_y(1))
        share(("below", q), below, q)
        q = down_order[n]
        down[q].wait_recv()
        if n < 4:
            pass_down[q] = send(amp.at[above, rows_of(q)], amp.at[above, rows_of(q)], at_y(3))
        share(("above", q), above, q)

    def y_last(n):
        far = column_of(2, k)
        q = up_order[n]
        pass_up[q].wait_recv()
        share(("far", q), far, q)
        q = down_order[n]
        pass_down[q].wait_recv()
        share(("far", q), far, q)

    def locate(source):
        count = jnp.int32(0)
        for j in range(4):
            for i in range(8):
                flag = flags[col * 8 + i, source * 4 + j]
                table[i, source * 4 + j] = PIECES + flag * (3 * count - PIECES)
                count = count + flag

    def pack():
        turned[...] = x_ref[...].T
        lane, short = lanes_of(TILE), lanes_of(PIECE)
        for j in range(4):
            rows = slice(j * TILE, (j + 1) * TILE)
            for i in range(8):
                first, offset = divmod(i * TILE, 128)
                tile = turned[rows, first * 128 : first * 128 + 128]
                if offset > 32:
                    right = turned[rows, first * 128 + 128 : first * 128 + 256]
                    tile = jnp.where(lane < offset, right, tile)
                spare = (offset + 96) % 128
                free = (short >= spare) & (short < spare + 32)
                last = tile[3 * PIECE :]
                for q in range(3):
                    piece = tile[q * PIECE : (q + 1) * PIECE]
                    tiles[3 * (8 * j + i) + q] = jnp.where(free, pltpu.roll(last, 96 - 32 * q, 1), piece)

        @pl.loop(0, CAP)
        def _(t):
            chosen = jnp.int32(0)
            for j in range(4):
                for i in range(8):
                    away = table[i, row * 4 + j] - 3 * t
                    chosen = chosen + (8 * j + i) * (1 - jnp.minimum(jnp.maximum(away, -away), 1))
            for q in range(3):
                blocks[0, 0][3 * t + q] = tiles[3 * chosen + q]

    lane24, lane96 = lanes_of(PIECE), lanes_of(TILE)

    def unpack(dx, dz):
        block = blocks[dx, dz]
        xs, zs = lax.rem(x + dx, 4), lax.rem(z + dz, 4)
        source = zs * 4 + xs
        column = lax.div(source, 2)
        base = lax.rem(source, 2) * 384

        @pl.loop(0, 4)
        def _(j):
            target = pl.ds(pl.multiple_of(base + j * TILE, 32), TILE)
            for group in range(2):
                parts = []
                for i in range(4):
                    start = table[group * 4 + i, source * 4 + j]
                    pieces = [block[start + q] for q in range(3)]
                    moved = [pltpu.roll(pieces[q], 32 + 32 * q, 1) for q in range(3)]
                    part_of = [(lane24 >= (q - i) % 4 * 32) & (lane24 < (q - i) % 4 * 32 + 32) for q in range(2)]
                    last = jnp.where(part_of[0], moved[0], jnp.where(part_of[1], moved[1], moved[2]))
                    parts.append(jnp.concatenate(pieces + [last], axis=0))
                for i in range(3):
                    high, low = split(jnp.where(lane96 < 96 - 32 * i, parts[i], parts[i + 1]))
                    lanes = pl.ds((group * 3 + i) * 128, 128)
                    b_high[column, target, lanes] = high
                    b_low[column, target, lanes] = low

    def product(column, left):
        a_high, a_low = split(left)
        high, low = b_high[column], b_low[column]
        return jnp.dot(
            jnp.concatenate([a_high, a_high, a_low], axis=1),
            jnp.concatenate([high, low, high], axis=0),
            preferred_element_type=jnp.float32,
        )

    near = lax.div(x, 2)

    def multiply(dz, core, half, wanted):
        zs = lax.rem(z + dz, 4)
        dy = lax.rem(zs + 4 - y, 4)
        first = (dy == 0) | ((dy == 3) & (half == 0)) | ((dy == 1) & (half == 1))

        @pl.when(wanted(dy, first))
        def _():
            rows = pl.ds(pl.multiple_of(half * 384, 384), 384)
            column = zs * 2 + core
            out_ref[rows, :] += product(column, amp[column, rows, :])

    locate(row)
    own_x.wait()
    pack()
    for block in blocks.values():
        block[PIECES:] = jnp.zeros((3, PIECE, 128), jnp.float32)
    out_ref[...] = jnp.zeros_like(out_ref)

    for half in halves:
        ring_send(half, 1, 0)
    for half in halves:
        ring_send(half, 2, 0)

    @pl.loop(0, 16)
    def _(source):
        locate(source)

    unpack(0, 0)
    y_step(0)
    for half in halves:
        ring_pass(half, 1, 0)
    for other in (3, 1):
        for half in halves:
            ring_send(half, 2, other)
    y_step(1)
    for half in halves:
        ring_pass(half, 2, 0)
    for key in ((0, 3), (0, 1), (3, 0), (1, 0)):
        unpack(*key)
    y_step(2)
    for half in halves:
        ring_last(half, 1, 0)
    for half in halves:
        ring_send(half, 2, 2)
    y_step(3)
    for half in halves:
        ring_pass(half, 2, 3)
    unpack(3, 3)
    y_step(4)
    for half in halves:
        ring_pass(half, 2, 1)
    for key in ((3, 1), (1, 3), (1, 1)):
        unpack(*key)
    y_step(5)
    own_amp.wait()
    shared["own"].wait_recv()
    for q in range(4):
        shared["below", q].wait_recv()
        shared["above", q + 4].wait_recv()

    @pl.loop(0, 6)
    def _(n):
        multiply(lax.rem(3 + lax.div(n, 2), 4), near, lax.rem(n, 2), lambda dy, first: first)

    for half in halves:
        ring_pass(half, 2, 2)
    y_step(6)
    for half in halves:
        ring_last(half, 2, 0)
    unpack(2, 0)
    unpack(0, 2)
    y_step(7)
    for half in halves:
        ring_last(half, 2, 3)
    unpack(2, 3)
    unpack(3, 2)
    for q in range(4):
        shared["below", q + 4].wait_recv()
        shared["above", q].wait_recv()

    @pl.loop(0, 10)
    def _(n):
        entry = lax.div(n, 2)
        done = entry < 3
        core = jnp.where(entry < 3, near, 1 - near)
        multiply(
            lax.rem(3 + lax.rem(entry, 3), 4), core, lax.rem(n, 2),
            lambda dy, first: (dy != 2) & jnp.logical_not(done & first))

    for half in halves:
        ring_last(half, 2, 1)
    unpack(2, 1)
    unpack(1, 2)
    y_last(0)

    @pl.loop(0, 4)
    def _(n):
        entry = lax.div(n, 2)
        core = jnp.where(entry == 0, near, 1 - near)
        multiply(2 - entry, core, lax.rem(n, 2), lambda dy, first: dy != 2)

    for half in halves:
        ring_last(half, 2, 2)
    unpack(2, 2)
    y_last(1)

    @pl.loop(0, 2)
    def _(n):
        multiply(jnp.int32(2), 1 - near, n, lambda dy, first: dy != 2)

    def finish(since, until, column):
        size = (until - since) * CHUNK
        rows = [pl.ds(order[since] * CHUNK, size) for order in (up_order, down_order)]
        value = product(column, jnp.concatenate([amp[column, r, :] for r in rows], axis=0))
        out_ref[rows[0], :] += value[:size]
        out_ref[rows[1], :] += value[size:]

    def finish_shared(since, until):
        for n in range(since, until):
            for q in (up_order[n], down_order[n]):
                shared["far", q].wait_recv()
        finish(since, until, column_of(2, 1 - k))

    y_last(2)
    finish(0, 3, column_of(2, k))
    finish_shared(0, 3)
    y_last(3)
    finish(3, 4, column_of(2, k))
    finish_shared(3, 4)
    for copy in started:
        copy.wait_send()


COPIES = 2 * CHUNKS + 1 + CHUNKS + 3 * CHUNKS + 40


def body(amplitudes, integrals, flags):
    return pl.pallas_call(
        main_kernel,
        out_shape=pltpu.VMEM((768, 768), jnp.float32),
        in_specs=[
            pl.BlockSpec(memory_space=pltpu.SMEM),
            pl.BlockSpec(memory_space=pl.ANY),
            pl.BlockSpec(memory_space=pl.ANY),
        ],
        out_specs=pl.BlockSpec(memory_space=pltpu.VMEM),
        scratch_shapes=[
            pltpu.VMEM((8, 768, 768), jnp.float32),
            pltpu.VMEM((8, 768, 768), jnp.bfloat16),
            pltpu.VMEM((8, 768, 768), jnp.bfloat16),
            pltpu.VMEM((768, 384), jnp.float32),
            pltpu.VMEM((384, 768), jnp.float32),
            pltpu.VMEM((96, PIECE, 128), jnp.float32),
            pltpu.SMEM((8, 64), jnp.int32),
        ]
        + [pltpu.VMEM((PIECES + 3, PIECE, 128), jnp.float32)] * 16
        + [
            pltpu.SemaphoreType.DMA((COPIES,)),
            pltpu.SemaphoreType.DMA((COPIES,)),
            pltpu.SemaphoreType.DMA((2,)),
        ],
        compiler_params=pltpu.CompilerParams(
            collective_id=0, has_side_effects=True, vmem_limit_bytes=62_000_000
        ),
        name="ladder",
    )(flags, amplitudes, integrals)


def solution(mesh):
    return jax.shard_map(
        body,
        mesh=mesh,
        in_specs=(P("row", "col"), P("col", "row"), P()),
        out_specs=P("row", "col"),
        check_vma=False,
    )
```

```python
import jax
import jax.numpy as jnp
from jax import lax
from jax.experimental import pallas as pl
from jax.experimental.pallas import tpu as pltpu
from jax.sharding import PartitionSpec as P

TILE = 96
CAP = 19
PIECE = 24
PIECES = 3 * CAP
MESH = pl.DeviceIdType.MESH
STARTS = (0, 224, 336, 384, 608, 720, 768)
CHUNKS = 6

FIRST, SECOND = (0, 29), (29, 28)
PASS_UP = {FIRST: (0, 14), SECOND: (29, 14)}
PASS_DOWN = {FIRST: (14, 15), SECOND: (43, 14)}


def lanes_of(rows):
    return lax.broadcasted_iota(jnp.int32, (rows, 128), 1)


def split(value):
    high = value.astype(jnp.bfloat16)
    low = (value - high.astype(jnp.float32)).astype(jnp.bfloat16)
    return high, low


def main_kernel(flags_hbm, amp_hbm, x_hbm, out_ref, amp, b_high, b_low, x_ref, turned, tiles, flags, table, *rest):
    blocks = {(dx, dz): rest[dx * 4 + dz] for dx in range(4) for dz in range(4)}
    send_sem, recv_sem, local_sem = rest[16:]
    row, col = lax.axis_index("row"), lax.axis_index("col")
    x, z = lax.rem(row, 4), lax.div(row, 4)
    k, y = lax.rem(col, 2), lax.div(col, 2)

    def at_x(d):
        return (z * 4 + lax.rem(x + d, 4), col)

    def at_z(d):
        return (lax.rem(z + d, 4) * 4 + x, col)

    def at_y(d):
        return (row, lax.rem(y + d, 4) * 2 + k)

    mate = (row, y * 2 + 1 - k)

    def column_of(d, core):
        return lax.rem(y + d, 4) * 2 + core

    own_flags = pltpu.make_async_copy(flags_hbm, flags, local_sem.at[2])
    own_flags.start()
    own_x = pltpu.make_async_copy(x_hbm, x_ref, local_sem.at[1])
    own_x.start()
    own_amp = pltpu.make_async_copy(amp_hbm, amp.at[col], local_sem.at[0])
    own_amp.start()

    barrier = pltpu.get_barrier_semaphore()
    for peer in (at_x(1), at_x(3), at_z(1), at_z(3), at_y(1), at_y(3), mate):
        pl.semaphore_signal(barrier, inc=1, device_id=peer, device_id_type=MESH)
    pl.semaphore_wait(barrier, 7)

    started = []

    def send(src, dst, device):
        n = len(started)
        copy = pltpu.make_async_remote_copy(
            src_ref=src, dst_ref=dst, send_sem=send_sem.at[n], recv_sem=recv_sem.at[n],
            device_id=device, device_id_type=MESH,
        )
        copy.start()
        started.append(copy)
        return copy

    def rows_of(q):
        return pl.ds(STARTS[q], STARTS[q + 1] - STARTS[q])

    up, down, pass_up, pass_down, shared = {}, {}, {}, {}, {}
    up_order, down_order = (0, 1, 2, 3, 4, 5), (3, 4, 5, 0, 1, 2)

    def send_own(n):
        q = up_order[n]
        up[q] = send(amp_hbm.at[rows_of(q)], amp.at[col, rows_of(q)], at_y(1))
        q = down_order[n]
        down[q] = send(amp_hbm.at[rows_of(q)], amp.at[col, rows_of(q)], at_y(3))

    def part(ref, span):
        return ref.at[pl.ds(span[0], span[1])]

    ring = {}

    def key_of(half, phase, other, d):
        along_x = (half is FIRST) == (phase == 1)
        return (d, other) if along_x else (other, d)

    def peer_of(half, phase, d):
        return at_x(d) if (half is FIRST) == (phase == 1) else at_z(d)

    def ring_send(half, phase, other):
        src = blocks[key_of(half, phase, other, 0)]
        ring[half, phase, other, "up"] = send(
            part(src, half), part(blocks[key_of(half, phase, other, 3)], half), peer_of(half, phase, 1))
        ring[half, phase, other, "down"] = send(
            part(src, half), part(blocks[key_of(half, phase, other, 1)], half), peer_of(half, phase, 3))

    def ring_pass(half, phase, other):
        ring[half, phase, other, "up"].wait_recv()
        far = blocks[key_of(half, phase, other, 2)]
        span = PASS_UP[half]
        ring[half, phase, other, "pass_up"] = send(
            part(blocks[key_of(half, phase, other, 3)], span), part(far, span), peer_of(half, phase, 1))
        ring[half, phase, other, "down"].wait_recv()
        span = PASS_DOWN[half]
        ring[half, phase, other, "pass_down"] = send(
            part(blocks[key_of(half, phase, other, 1)], span), part(far, span), peer_of(half, phase, 3))

    def ring_last(half, phase, other):
        ring[half, phase, other, "pass_up"].wait_recv()
        ring[half, phase, other, "pass_down"].wait_recv()

    halves = (FIRST, SECOND)

    for n in range(CHUNKS):
        send_own(n)
    shared["own"] = send(amp_hbm, amp.at[col], mate)

    def share(key, column, q):
        shared[key] = send(amp.at[column, rows_of(q)], amp.at[column, rows_of(q)], mate)

    def y_step(n):
        below, above = column_of(3, k), column_of(1, k)
        q = up_order[n]
        up[q].wait_recv()
        if n < 3:
            pass_up[q] = send(amp.at[below, rows_of(q)], amp.at[below, rows_of(q)], at_y(1))
        share(("below", q), below, q)
        q = down_order[n]
        down[q].wait_recv()
        if n < 3:
            pass_down[q] = send(amp.at[above, rows_of(q)], amp.at[above, rows_of(q)], at_y(3))
        share(("above", q), above, q)

    def y_last(n):
        far = column_of(2, k)
        q = up_order[n]
        pass_up[q].wait_recv()
        share(("far", q), far, q)
        q = down_order[n]
        pass_down[q].wait_recv()
        share(("far", q), far, q)

    def locate(source):
        count = jnp.int32(0)
        for j in range(4):
            for i in range(8):
                flag = flags[col * 8 + i, source * 4 + j]
                table[i, source * 4 + j] = PIECES + flag * (3 * count - PIECES)
                count = count + flag

    def pack():
        turned[...] = x_ref[...].T
        lane, short = lanes_of(TILE), lanes_of(PIECE)
        for j in range(4):
            rows = slice(j * TILE, (j + 1) * TILE)
            for i in range(8):
                first, offset = divmod(i * TILE, 128)
                tile = turned[rows, first * 128 : first * 128 + 128]
                if offset > 32:
                    right = turned[rows, first * 128 + 128 : first * 128 + 256]
                    tile = jnp.where(lane < offset, right, tile)
                spare = (offset + 96) % 128
                free = (short >= spare) & (short < spare + 32)
                last = tile[3 * PIECE :]
                for q in range(3):
                    piece = tile[q * PIECE : (q + 1) * PIECE]
                    tiles[3 * (8 * j + i) + q] = jnp.where(free, pltpu.roll(last, 96 - 32 * q, 1), piece)

        @pl.loop(0, CAP)
        def _(t):
            chosen = jnp.int32(0)
            for j in range(4):
                for i in range(8):
                    away = table[i, row * 4 + j] - 3 * t
                    chosen = chosen + (8 * j + i) * (1 - jnp.minimum(jnp.maximum(away, -away), 1))
            for q in range(3):
                blocks[0, 0][3 * t + q] = tiles[3 * chosen + q]

    lane24, lane96 = lanes_of(PIECE), lanes_of(TILE)

    def unpack(dx, dz):
        block = blocks[dx, dz]
        xs, zs = lax.rem(x + dx, 4), lax.rem(z + dz, 4)
        source = zs * 4 + xs
        column = lax.div(source, 2)
        base = lax.rem(source, 2) * 384

        @pl.loop(0, 4)
        def _(j):
            target = pl.ds(pl.multiple_of(base + j * TILE, 32), TILE)
            for group in range(2):
                parts = []
                for i in range(4):
                    start = table[group * 4 + i, source * 4 + j]
                    pieces = [block[start + q] for q in range(3)]
                    moved = [pltpu.roll(pieces[q], 32 + 32 * q, 1) for q in range(3)]
                    part_of = [(lane24 >= (q - i) % 4 * 32) & (lane24 < (q - i) % 4 * 32 + 32) for q in range(2)]
                    last = jnp.where(part_of[0], moved[0], jnp.where(part_of[1], moved[1], moved[2]))
                    parts.append(jnp.concatenate(pieces + [last], axis=0))
                for i in range(3):
                    high, low = split(jnp.where(lane96 < 96 - 32 * i, parts[i], parts[i + 1]))
                    lanes = pl.ds((group * 3 + i) * 128, 128)
                    b_high[column, target, lanes] = high
                    b_low[column, target, lanes] = low

    def product(column, left, depth=slice(None)):
        a_high, a_low = split(left)
        high, low = b_high[column, depth, :], b_low[column, depth, :]
        return jnp.dot(
            jnp.concatenate([a_high, a_high, a_low], axis=1),
            jnp.concatenate([high, low, high], axis=0),
            preferred_element_type=jnp.float32,
        )

    near = lax.div(x, 2)
    far = 1 - near
    same = pl.ds(pl.multiple_of(lax.rem(x, 2) * 384, 128), 384)
    other_block = pl.ds(pl.multiple_of((1 - lax.rem(x, 2)) * 384, 128), 384)

    def multiply(dz, core, half, whole=None, block=None, partly=None):
        zs = lax.rem(z + dz, 4)
        dy = lax.rem(zs + 4 - y, 4)
        first = (dy == 0) | ((dy == 3) & (half == 0)) | ((dy == 1) & (half == 1))
        rows = pl.ds(pl.multiple_of(half * 384, 384), 384)
        column = zs * 2 + core
        if whole is not None:

            @pl.when(whole(dy, first))
            def _():
                out_ref[rows, :] += product(column, amp[column, rows, :])

        if block is not None:

            @pl.when(partly(dy, first))
            def _():
                out_ref[rows, :] += product(column, amp[column, rows, block], block)

    def early(dy, first):
        return first

    def late(dy, first):
        return (dy != 2) & jnp.logical_not(first)

    own_flags.wait()
    locate(row)
    own_x.wait()
    pack()
    for block in blocks.values():
        block[PIECES:] = jnp.zeros((3, PIECE, 128), jnp.float32)
    out_ref[...] = jnp.zeros_like(out_ref)

    for half in halves:
        ring_send(half, 1, 0)
    for half in halves:
        ring_send(half, 2, 0)

    @pl.loop(0, 16)
    def _(source):
        locate(source)

    unpack(0, 0)
    for half in halves:
        ring_pass(half, 1, 0)
    for other in (3, 1):
        for half in halves:
            ring_send(half, 2, other)
    y_step(0)
    for half in halves:
        ring_pass(half, 2, 0)
    for key in ((0, 3), (0, 1), (3, 0), (1, 0)):
        unpack(*key)
    for half in halves:
        ring_last(half, 1, 0)
    for half in halves:
        ring_send(half, 2, 2)
    y_step(1)
    y_step(2)
    for half in halves:
        ring_pass(half, 2, 3)
    unpack(3, 3)
    for half in halves:
        ring_pass(half, 2, 1)
    for key in ((3, 1), (1, 3), (1, 1)):
        unpack(*key)
    y_step(3)
    own_amp.wait()
    shared["own"].wait_recv()
    for q in range(3):
        shared["below", q].wait_recv()
        shared["above", q + 3].wait_recv()

    @pl.loop(0, 6)
    def _(n):
        multiply(lax.rem(3 + lax.div(n, 2), 4), near, lax.rem(n, 2), early)

    for half in halves:
        ring_pass(half, 2, 2)
    y_step(4)

    @pl.loop(0, 6)
    def _(n):
        multiply(lax.rem(3 + lax.div(n, 2), 4), far, lax.rem(n, 2), None, other_block, early)

    for half in halves:
        ring_last(half, 2, 0)
    unpack(2, 0)
    unpack(0, 2)

    @pl.loop(0, 4)
    def _(n):
        entry = lax.div(n, 2)
        multiply(2 * entry, jnp.where(entry == 0, far, near), lax.rem(n, 2), None, same, early)

    y_step(5)
    for half in halves:
        ring_last(half, 2, 3)
    unpack(2, 3)
    unpack(3, 2)
    for q in range(3):
        shared["below", q + 3].wait_recv()
        shared["above", q].wait_recv()

    @pl.loop(0, 8)
    def _(n):
        entry = lax.div(n, 2)
        core = jnp.where(entry < 3, near, far)
        multiply(lax.rem(3 + entry, 4) * jnp.where(entry < 3, 1, 0), core, lax.rem(n, 2), late)

    @pl.loop(0, 2)
    def _(n):
        multiply(jnp.int32(3), far, n, late, same, early)

    for half in halves:
        ring_last(half, 2, 1)
    unpack(2, 1)
    unpack(1, 2)

    @pl.loop(0, 4)
    def _(n):
        entry = lax.div(n, 2)
        core = jnp.where(entry == 0, near, far)
        block = pl.ds(pl.multiple_of(jnp.where(entry == 0, other_block.start, same.start), 128), 384)
        multiply(2 - entry, core, lax.rem(n, 2), late, block, early)

    for half in halves:
        ring_last(half, 2, 2)
    unpack(2, 2)
    y_last(0)

    @pl.loop(0, 2)
    def _(n):
        multiply(jnp.int32(2), 1 - near, n, lambda dy, first: dy != 2)

    def finish(n, column):
        rows = [rows_of(q) for q in (up_order[n], down_order[n])]
        size = rows[0].size
        a_high, a_low = split(jnp.concatenate([amp[column, r, :] for r in rows], axis=0))
        value = jnp.dot(
            jnp.concatenate([a_high, a_low], axis=0), b_high[column], preferred_element_type=jnp.float32)
        value = value[: 2 * size] + value[2 * size :]
        value += jnp.dot(a_high, b_low[column], preferred_element_type=jnp.float32)
        out_ref[rows[0], :] += value[:size]
        out_ref[rows[1], :] += value[size:]

    def finish_shared(n):
        for q in (up_order[n], down_order[n]):
            shared["far", q].wait_recv()
        finish(n, column_of(2, 1 - k))

    finish(0, column_of(2, k))
    y_last(1)
    finish_shared(0)
    finish(1, column_of(2, k))
    y_last(2)
    finish_shared(1)
    finish(2, column_of(2, k))
    finish_shared(2)
    for copy in started:
        copy.wait_send()


COPIES = 2 * CHUNKS + 1 + CHUNKS + 3 * CHUNKS + 40


def body(amplitudes, integrals, flags):
    return pl.pallas_call(
        main_kernel,
        out_shape=pltpu.VMEM((768, 768), jnp.float32),
        in_specs=[
            pl.BlockSpec(memory_space=pl.ANY),
            pl.BlockSpec(memory_space=pl.ANY),
            pl.BlockSpec(memory_space=pl.ANY),
        ],
        out_specs=pl.BlockSpec(memory_space=pltpu.VMEM),
        scratch_shapes=[
            pltpu.VMEM((8, 768, 768), jnp.float32),
            pltpu.VMEM((8, 768, 768), jnp.bfloat16),
            pltpu.VMEM((8, 768, 768), jnp.bfloat16),
            pltpu.VMEM((768, 384), jnp.float32),
            pltpu.VMEM((384, 768), jnp.float32),
            pltpu.VMEM((96, PIECE, 128), jnp.float32),
            pltpu.SMEM((64, 64), jnp.int32),
            pltpu.SMEM((8, 64), jnp.int32),
        ]
        + [pltpu.VMEM((PIECES + 3, PIECE, 128), jnp.float32)] * 16
        + [
            pltpu.SemaphoreType.DMA((COPIES,)),
            pltpu.SemaphoreType.DMA((COPIES,)),
            pltpu.SemaphoreType.DMA((3,)),
        ],
        compiler_params=pltpu.CompilerParams(
            collective_id=0, has_side_effects=True, vmem_limit_bytes=62_000_000
        ),
        name="ladder",
    )(flags, amplitudes, integrals)


def solution(mesh):
    return jax.shard_map(
        body,
        mesh=mesh,
        in_specs=(P("row", "col"), P("col", "row"), P()),
        out_specs=P("row", "col"),
        check_vma=False,
    )
```

```python
import jax
import jax.numpy as jnp
from jax import lax
from jax.experimental import pallas as pl
from jax.experimental.pallas import tpu as pltpu
from jax.sharding import PartitionSpec as P

TILE = 96
CAP = 19
PIECE = 24
PIECES = 3 * CAP
MESH = pl.DeviceIdType.MESH
STARTS = (0, 208, 320, 384, 592, 704, 768)
CHUNKS = 6

FIRST, SECOND = (0, 29), (29, 28)
PASS_UP = {FIRST: (0, 14), SECOND: (29, 14)}
PASS_DOWN = {FIRST: (14, 15), SECOND: (43, 14)}


def lanes_of(rows):
    return lax.broadcasted_iota(jnp.int32, (rows, 128), 1)


def split(value):
    high = value.astype(jnp.bfloat16)
    low = (value - high.astype(jnp.float32)).astype(jnp.bfloat16)
    return high, low


def main_kernel(flags_hbm, amp_hbm, x_hbm, out_ref, amp, b_high, b_low, x_ref, turned, tiles, flags, table, *rest):
    blocks = {(dx, dz): rest[dx * 4 + dz] for dx in range(4) for dz in range(4)}
    send_sem, recv_sem, local_sem = rest[16:]
    row, col = lax.axis_index("row"), lax.axis_index("col")
    x, z = lax.rem(row, 4), lax.div(row, 4)
    k, y = lax.rem(col, 2), lax.div(col, 2)

    def at_x(d):
        return (z * 4 + lax.rem(x + d, 4), col)

    def at_z(d):
        return (lax.rem(z + d, 4) * 4 + x, col)

    def at_y(d):
        return (row, lax.rem(y + d, 4) * 2 + k)

    mate = (row, y * 2 + 1 - k)

    def column_of(d, core):
        return lax.rem(y + d, 4) * 2 + core

    own_flags = pltpu.make_async_copy(flags_hbm, flags, local_sem.at[2])
    own_flags.start()
    own_x = pltpu.make_async_copy(x_hbm, x_ref, local_sem.at[1])
    own_x.start()
    own_amp = pltpu.make_async_copy(amp_hbm, amp.at[col], local_sem.at[0])
    own_amp.start()

    barrier = pltpu.get_barrier_semaphore()
    for peer in (at_x(1), at_x(3), at_z(1), at_z(3), at_y(1), at_y(3), mate):
        pl.semaphore_signal(barrier, inc=1, device_id=peer, device_id_type=MESH)
    pl.semaphore_wait(barrier, 7)

    started = []

    def send(src, dst, device):
        n = len(started)
        copy = pltpu.make_async_remote_copy(
            src_ref=src, dst_ref=dst, send_sem=send_sem.at[n], recv_sem=recv_sem.at[n],
            device_id=device, device_id_type=MESH,
        )
        copy.start()
        started.append(copy)
        return copy

    def rows_of(q):
        return pl.ds(STARTS[q], STARTS[q + 1] - STARTS[q])

    up, down, pass_up, pass_down, shared = {}, {}, {}, {}, {}
    up_order, down_order = (0, 1, 2, 3, 4, 5), (3, 4, 5, 0, 1, 2)

    def send_own(n):
        q = up_order[n]
        up[q] = send(amp_hbm.at[rows_of(q)], amp.at[col, rows_of(q)], at_y(1))
        q = down_order[n]
        down[q] = send(amp_hbm.at[rows_of(q)], amp.at[col, rows_of(q)], at_y(3))

    def part(ref, span):
        return ref.at[pl.ds(span[0], span[1])]

    ring = {}

    def key_of(half, phase, other, d):
        along_x = (half is FIRST) == (phase == 1)
        return (d, other) if along_x else (other, d)

    def peer_of(half, phase, d):
        return at_x(d) if (half is FIRST) == (phase == 1) else at_z(d)

    def ring_send(half, phase, other):
        src = blocks[key_of(half, phase, other, 0)]
        ring[half, phase, other, "up"] = send(
            part(src, half), part(blocks[key_of(half, phase, other, 3)], half), peer_of(half, phase, 1))
        ring[half, phase, other, "down"] = send(
            part(src, half), part(blocks[key_of(half, phase, other, 1)], half), peer_of(half, phase, 3))

    def ring_pass(half, phase, other):
        ring[half, phase, other, "up"].wait_recv()
        far = blocks[key_of(half, phase, other, 2)]
        span = PASS_UP[half]
        ring[half, phase, other, "pass_up"] = send(
            part(blocks[key_of(half, phase, other, 3)], span), part(far, span), peer_of(half, phase, 1))
        ring[half, phase, other, "down"].wait_recv()
        span = PASS_DOWN[half]
        ring[half, phase, other, "pass_down"] = send(
            part(blocks[key_of(half, phase, other, 1)], span), part(far, span), peer_of(half, phase, 3))

    def ring_last(half, phase, other):
        ring[half, phase, other, "pass_up"].wait_recv()
        ring[half, phase, other, "pass_down"].wait_recv()

    halves = (FIRST, SECOND)

    for n in range(CHUNKS):
        send_own(n)
    shared["own"] = send(amp_hbm, amp.at[col], mate)

    def share(key, column, q):
        shared[key] = send(amp.at[column, rows_of(q)], amp.at[column, rows_of(q)], mate)

    def y_step(n):
        below, above = column_of(3, k), column_of(1, k)
        q = up_order[n]
        up[q].wait_recv()
        if n < 3:
            pass_up[q] = send(amp.at[below, rows_of(q)], amp.at[below, rows_of(q)], at_y(1))
        share(("below", q), below, q)
        q = down_order[n]
        down[q].wait_recv()
        if n < 3:
            pass_down[q] = send(amp.at[above, rows_of(q)], amp.at[above, rows_of(q)], at_y(3))
        share(("above", q), above, q)

    def y_last(n):
        far = column_of(2, k)
        q = up_order[n]
        pass_up[q].wait_recv()
        share(("far", q), far, q)
        q = down_order[n]
        pass_down[q].wait_recv()
        share(("far", q), far, q)

    def locate(source):
        count = jnp.int32(0)
        for j in range(4):
            for i in range(8):
                flag = flags[col * 8 + i, source * 4 + j]
                table[i, source * 4 + j] = PIECES + flag * (3 * count - PIECES)
                count = count + flag

    def pack():
        turned[...] = x_ref[...].T
        lane, short = lanes_of(TILE), lanes_of(PIECE)
        for j in range(4):
            rows = slice(j * TILE, (j + 1) * TILE)
            for i in range(8):
                first, offset = divmod(i * TILE, 128)
                tile = turned[rows, first * 128 : first * 128 + 128]
                if offset > 32:
                    right = turned[rows, first * 128 + 128 : first * 128 + 256]
                    tile = jnp.where(lane < offset, right, tile)
                spare = (offset + 96) % 128
                free = (short >= spare) & (short < spare + 32)
                last = tile[3 * PIECE :]
                for q in range(3):
                    piece = tile[q * PIECE : (q + 1) * PIECE]
                    tiles[3 * (8 * j + i) + q] = jnp.where(free, pltpu.roll(last, 96 - 32 * q, 1), piece)

        @pl.loop(0, CAP)
        def _(t):
            chosen = jnp.int32(0)
            for j in range(4):
                for i in range(8):
                    away = table[i, row * 4 + j] - 3 * t
                    chosen = chosen + (8 * j + i) * (1 - jnp.minimum(jnp.maximum(away, -away), 1))
            for q in range(3):
                blocks[0, 0][3 * t + q] = tiles[3 * chosen + q]

    lane24, lane96 = lanes_of(PIECE), lanes_of(TILE)

    def unpack(dx, dz):
        block = blocks[dx, dz]
        xs, zs = lax.rem(x + dx, 4), lax.rem(z + dz, 4)
        source = zs * 4 + xs
        column = lax.div(source, 2)
        base = lax.rem(source, 2) * 384

        @pl.loop(0, 4)
        def _(j):
            target = pl.ds(pl.multiple_of(base + j * TILE, 32), TILE)
            for group in range(2):
                parts = []
                for i in range(4):
                    start = table[group * 4 + i, source * 4 + j]
                    pieces = [block[start + q] for q in range(3)]
                    moved = [pltpu.roll(pieces[q], 32 + 32 * q, 1) for q in range(3)]
                    part_of = [(lane24 >= (q - i) % 4 * 32) & (lane24 < (q - i) % 4 * 32 + 32) for q in range(2)]
                    last = jnp.where(part_of[0], moved[0], jnp.where(part_of[1], moved[1], moved[2]))
                    parts.append(jnp.concatenate(pieces + [last], axis=0))
                for i in range(3):
                    high, low = split(jnp.where(lane96 < 96 - 32 * i, parts[i], parts[i + 1]))
                    lanes = pl.ds((group * 3 + i) * 128, 128)
                    b_high[column, target, lanes] = high
                    b_low[column, target, lanes] = low

    def product(column, left, depth=slice(None)):
        a_high, a_low = split(left)
        high, low = b_high[column, depth, :], b_low[column, depth, :]
        return jnp.dot(
            jnp.concatenate([a_high, a_high, a_low], axis=1),
            jnp.concatenate([high, low, high], axis=0),
            preferred_element_type=jnp.float32,
        )

    near = lax.div(x, 2)
    far = 1 - near
    same = pl.ds(pl.multiple_of(lax.rem(x, 2) * 384, 128), 384)
    other_block = pl.ds(pl.multiple_of((1 - lax.rem(x, 2)) * 384, 128), 384)

    def multiply(dz, core, half, whole=None, block=None, partly=None):
        zs = lax.rem(z + dz, 4)
        dy = lax.rem(zs + 4 - y, 4)
        first = (dy == 0) | ((dy == 3) & (half == 0)) | ((dy == 1) & (half == 1))
        rows = pl.ds(pl.multiple_of(half * 384, 384), 384)
        column = zs * 2 + core
        if whole is not None:

            @pl.when(whole(dy, first))
            def _():
                out_ref[rows, :] += product(column, amp[column, rows, :])

        if block is not None:

            @pl.when(partly(dy, first))
            def _():
                out_ref[rows, :] += product(column, amp[column, rows, block], block)

    def early(dy, first):
        return first

    def late(dy, first):
        return (dy != 2) & jnp.logical_not(first)

    own_flags.wait()
    locate(row)
    own_x.wait()
    pack()
    for block in blocks.values():
        block[PIECES:] = jnp.zeros((3, PIECE, 128), jnp.float32)
    out_ref[...] = jnp.zeros_like(out_ref)

    for half in halves:
        ring_send(half, 1, 0)
    for half in halves:
        ring_send(half, 2, 0)

    @pl.loop(0, 16)
    def _(source):
        locate(source)

    unpack(0, 0)
    for half in halves:
        ring_pass(half, 1, 0)
    for other in (3, 1):
        for half in halves:
            ring_send(half, 2, other)
    y_step(0)
    for half in halves:
        ring_pass(half, 2, 0)
    for key in ((0, 3), (0, 1), (3, 0), (1, 0)):
        unpack(*key)
    for half in halves:
        ring_last(half, 1, 0)
    for half in halves:
        ring_send(half, 2, 2)
    y_step(1)
    y_step(2)
    for half in halves:
        ring_pass(half, 2, 3)
    unpack(3, 3)
    for half in halves:
        ring_pass(half, 2, 1)
    for key in ((3, 1), (1, 3), (1, 1)):
        unpack(*key)
    y_step(3)
    own_amp.wait()
    shared["own"].wait_recv()
    for q in range(3):
        shared["below", q].wait_recv()
        shared["above", q + 3].wait_recv()

    @pl.loop(0, 6)
    def _(n):
        multiply(lax.rem(3 + lax.div(n, 2), 4), near, lax.rem(n, 2), early)

    for half in halves:
        ring_pass(half, 2, 2)
    y_step(4)

    @pl.loop(0, 6)
    def _(n):
        multiply(lax.rem(3 + lax.div(n, 2), 4), far, lax.rem(n, 2), None, other_block, early)

    for half in halves:
        ring_last(half, 2, 0)
    unpack(2, 0)
    unpack(0, 2)

    @pl.loop(0, 4)
    def _(n):
        entry = lax.div(n, 2)
        multiply(2 * entry, jnp.where(entry == 0, far, near), lax.rem(n, 2), None, same, early)

    y_step(5)
    for half in halves:
        ring_last(half, 2, 3)
    unpack(2, 3)
    unpack(3, 2)
    for q in range(3):
        shared["below", q + 3].wait_recv()
        shared["above", q].wait_recv()

    @pl.loop(0, 8)
    def _(n):
        entry = lax.div(n, 2)
        core = jnp.where(entry < 3, near, far)
        multiply(lax.rem(3 + entry, 4) * jnp.where(entry < 3, 1, 0), core, lax.rem(n, 2), late)

    @pl.loop(0, 2)
    def _(n):
        multiply(jnp.int32(3), far, n, late, same, early)

    for half in halves:
        ring_last(half, 2, 1)
    unpack(2, 1)
    unpack(1, 2)

    @pl.loop(0, 4)
    def _(n):
        entry = lax.div(n, 2)
        core = jnp.where(entry == 0, near, far)
        block = pl.ds(pl.multiple_of(jnp.where(entry == 0, other_block.start, same.start), 128), 384)
        multiply(2 - entry, core, lax.rem(n, 2), late, block, early)

    for half in halves:
        ring_last(half, 2, 2)
    unpack(2, 2)
    y_last(0)

    @pl.loop(0, 2)
    def _(n):
        multiply(jnp.int32(2), 1 - near, n, lambda dy, first: dy != 2)

    def finish(n, column):
        rows = [rows_of(q) for q in (up_order[n], down_order[n])]
        size = rows[0].size
        a_high, a_low = split(jnp.concatenate([amp[column, r, :] for r in rows], axis=0))
        value = jnp.dot(
            jnp.concatenate([a_high, a_low], axis=0), b_high[column], preferred_element_type=jnp.float32)
        value = value[: 2 * size] + value[2 * size :]
        value += jnp.dot(a_high, b_low[column], preferred_element_type=jnp.float32)
        out_ref[rows[0], :] += value[:size]
        out_ref[rows[1], :] += value[size:]

    def finish_shared(n):
        for q in (up_order[n], down_order[n]):
            shared["far", q].wait_recv()
        finish(n, column_of(2, 1 - k))

    finish(0, column_of(2, k))
    y_last(1)
    finish_shared(0)
    finish(1, column_of(2, k))
    y_last(2)
    finish_shared(1)
    finish(2, column_of(2, k))
    finish_shared(2)
    for copy in started:
        copy.wait_send()


COPIES = 2 * CHUNKS + 1 + CHUNKS + 3 * CHUNKS + 40


def body(amplitudes, integrals, flags):
    return pl.pallas_call(
        main_kernel,
        out_shape=pltpu.VMEM((768, 768), jnp.float32),
        in_specs=[
            pl.BlockSpec(memory_space=pl.ANY),
            pl.BlockSpec(memory_space=pl.ANY),
            pl.BlockSpec(memory_space=pl.ANY),
        ],
        out_specs=pl.BlockSpec(memory_space=pltpu.VMEM),
        scratch_shapes=[
            pltpu.VMEM((8, 768, 768), jnp.float32),
            pltpu.VMEM((8, 768, 768), jnp.bfloat16),
            pltpu.VMEM((8, 768, 768), jnp.bfloat16),
            pltpu.VMEM((768, 384), jnp.float32),
            pltpu.VMEM((384, 768), jnp.float32),
            pltpu.VMEM((96, PIECE, 128), jnp.float32),
            pltpu.SMEM((64, 64), jnp.int32),
            pltpu.SMEM((8, 64), jnp.int32),
        ]
        + [pltpu.VMEM((PIECES + 3, PIECE, 128), jnp.float32)] * 16
        + [
            pltpu.SemaphoreType.DMA((COPIES,)),
            pltpu.SemaphoreType.DMA((COPIES,)),
            pltpu.SemaphoreType.DMA((3,)),
        ],
        compiler_params=pltpu.CompilerParams(
            collective_id=0, has_side_effects=True, vmem_limit_bytes=62_000_000
        ),
        name="ladder",
    )(flags, amplitudes, integrals)


def solution(mesh):
    return jax.shard_map(
        body,
        mesh=mesh,
        in_specs=(P("row", "col"), P("col", "row"), P()),
        out_specs=P("row", "col"),
        check_vma=False,
    )
```

```python
import jax
import jax.numpy as jnp
from jax import lax
from jax.experimental import pallas as pl
from jax.experimental.pallas import tpu as pltpu
from jax.sharding import PartitionSpec as P

TILE = 96
CAP = 19
PIECE = 24
PIECES = 3 * CAP
MESH = pl.DeviceIdType.MESH
STARTS = (0, 208, 320, 384, 592, 704, 768)
CHUNKS = 6

FIRST, SECOND = (0, 29), (29, 28)
PASS_UP = {FIRST: (0, 14), SECOND: (29, 14)}
PASS_DOWN = {FIRST: (14, 15), SECOND: (43, 14)}


def lanes_of(rows):
    return lax.broadcasted_iota(jnp.int32, (rows, 128), 1)


def split(value):
    high = value.astype(jnp.bfloat16)
    low = (value - high.astype(jnp.float32)).astype(jnp.bfloat16)
    return high, low


def main_kernel(flags_hbm, amp_hbm, x_hbm, out_ref, amp, b_high, b_low, x_ref, turned, tiles, flags, table, *rest):
    blocks = {(dx, dz): rest[dx * 4 + dz] for dx in range(4) for dz in range(4)}
    send_sem, recv_sem, local_sem = rest[16:]
    row, col = lax.axis_index("row"), lax.axis_index("col")
    x, z = lax.rem(row, 4), lax.div(row, 4)
    k, y = lax.rem(col, 2), lax.div(col, 2)

    def at_x(d):
        return (z * 4 + lax.rem(x + d, 4), col)

    def at_z(d):
        return (lax.rem(z + d, 4) * 4 + x, col)

    def at_y(d):
        return (row, lax.rem(y + d, 4) * 2 + k)

    mate = (row, y * 2 + 1 - k)

    def column_of(d, core):
        return lax.rem(y + d, 4) * 2 + core

    own_flags = pltpu.make_async_copy(flags_hbm, flags, local_sem.at[2])
    own_flags.start()
    own_x = pltpu.make_async_copy(x_hbm, x_ref, local_sem.at[1])
    own_x.start()
    own_amp = pltpu.make_async_copy(amp_hbm, amp.at[col], local_sem.at[0])
    own_amp.start()

    barrier = pltpu.get_barrier_semaphore()
    for peer in (at_x(1), at_x(3), at_z(1), at_z(3), at_y(1), at_y(3), mate):
        pl.semaphore_signal(barrier, inc=1, device_id=peer, device_id_type=MESH)
    pl.semaphore_wait(barrier, 7)

    started = []

    def send(src, dst, device):
        n = len(started)
        copy = pltpu.make_async_remote_copy(
            src_ref=src, dst_ref=dst, send_sem=send_sem.at[n], recv_sem=recv_sem.at[n],
            device_id=device, device_id_type=MESH,
        )
        copy.start()
        started.append(copy)
        return copy

    def rows_of(q):
        return pl.ds(STARTS[q], STARTS[q + 1] - STARTS[q])

    up, down, pass_up, pass_down, shared = {}, {}, {}, {}, {}
    up_order, down_order = (0, 1, 2, 3, 4, 5), (3, 4, 5, 0, 1, 2)

    def send_own(n):
        q = up_order[n]
        up[q] = send(amp_hbm.at[rows_of(q)], amp.at[col, rows_of(q)], at_y(1))
        q = down_order[n]
        down[q] = send(amp_hbm.at[rows_of(q)], amp.at[col, rows_of(q)], at_y(3))

    def part(ref, span):
        return ref.at[pl.ds(span[0], span[1])]

    ring = {}

    def key_of(half, phase, other, d):
        along_x = (half is FIRST) == (phase == 1)
        return (d, other) if along_x else (other, d)

    def peer_of(half, phase, d):
        return at_x(d) if (half is FIRST) == (phase == 1) else at_z(d)

    def ring_send(half, phase, other):
        src = blocks[key_of(half, phase, other, 0)]
        ring[half, phase, other, "up"] = send(
            part(src, half), part(blocks[key_of(half, phase, other, 3)], half), peer_of(half, phase, 1))
        ring[half, phase, other, "down"] = send(
            part(src, half), part(blocks[key_of(half, phase, other, 1)], half), peer_of(half, phase, 3))

    def ring_pass(half, phase, other):
        ring[half, phase, other, "up"].wait_recv()
        far = blocks[key_of(half, phase, other, 2)]
        span = PASS_UP[half]
        ring[half, phase, other, "pass_up"] = send(
            part(blocks[key_of(half, phase, other, 3)], span), part(far, span), peer_of(half, phase, 1))
        ring[half, phase, other, "down"].wait_recv()
        span = PASS_DOWN[half]
        ring[half, phase, other, "pass_down"] = send(
            part(blocks[key_of(half, phase, other, 1)], span), part(far, span), peer_of(half, phase, 3))

    def ring_last(half, phase, other):
        ring[half, phase, other, "pass_up"].wait_recv()
        ring[half, phase, other, "pass_down"].wait_recv()

    halves = (FIRST, SECOND)

    for n in range(CHUNKS):
        send_own(n)
    shared["own"] = send(amp_hbm, amp.at[col], mate)

    def share(key, column, q):
        shared[key] = send(amp.at[column, rows_of(q)], amp.at[column, rows_of(q)], mate)

    def y_step(n):
        below, above = column_of(3, k), column_of(1, k)
        q = up_order[n]
        up[q].wait_recv()
        if n < 3:
            pass_up[q] = send(amp.at[below, rows_of(q)], amp.at[below, rows_of(q)], at_y(1))
        share(("below", q), below, q)
        q = down_order[n]
        down[q].wait_recv()
        if n < 3:
            pass_down[q] = send(amp.at[above, rows_of(q)], amp.at[above, rows_of(q)], at_y(3))
        share(("above", q), above, q)

    def y_last(n):
        far = column_of(2, k)
        q = up_order[n]
        pass_up[q].wait_recv()
        share(("far", q), far, q)
        q = down_order[n]
        pass_down[q].wait_recv()
        share(("far", q), far, q)

    def locate(source):
        count = jnp.int32(0)
        for j in range(4):
            for i in range(8):
                flag = flags[col * 8 + i, source * 4 + j]
                table[i, source * 4 + j] = PIECES + flag * (3 * count - PIECES)
                count = count + flag

    def pack():
        turned[...] = x_ref[...].T
        lane, short = lanes_of(TILE), lanes_of(PIECE)
        for j in range(4):
            rows = slice(j * TILE, (j + 1) * TILE)
            for i in range(8):
                first, offset = divmod(i * TILE, 128)
                tile = turned[rows, first * 128 : first * 128 + 128]
                if offset > 32:
                    right = turned[rows, first * 128 + 128 : first * 128 + 256]
                    tile = jnp.where(lane < offset, right, tile)
                spare = (offset + 96) % 128
                free = (short >= spare) & (short < spare + 32)
                last = tile[3 * PIECE :]
                for q in range(3):
                    piece = tile[q * PIECE : (q + 1) * PIECE]
                    tiles[3 * (8 * j + i) + q] = jnp.where(free, pltpu.roll(last, 96 - 32 * q, 1), piece)

        @pl.loop(0, CAP, unroll=True)
        def _(t):
            chosen = jnp.int32(0)
            for j in range(4):
                for i in range(8):
                    away = table[i, row * 4 + j] - 3 * t
                    chosen = chosen + (8 * j + i) * (1 - jnp.minimum(jnp.maximum(away, -away), 1))
            for q in range(3):
                blocks[0, 0][3 * t + q] = tiles[3 * chosen + q]

    lane24, lane96 = lanes_of(PIECE), lanes_of(TILE)

    def unpack(dx, dz):
        block = blocks[dx, dz]
        xs, zs = lax.rem(x + dx, 4), lax.rem(z + dz, 4)
        source = zs * 4 + xs
        column = lax.div(source, 2)
        base = lax.rem(source, 2) * 384

        @pl.loop(0, 4)
        def _(j):
            target = pl.ds(pl.multiple_of(base + j * TILE, 32), TILE)
            for group in range(2):
                parts = []
                for i in range(4):
                    start = table[group * 4 + i, source * 4 + j]
                    pieces = [block[start + q] for q in range(3)]
                    moved = [pltpu.roll(pieces[q], 32 + 32 * q, 1) for q in range(3)]
                    part_of = [(lane24 >= (q - i) % 4 * 32) & (lane24 < (q - i) % 4 * 32 + 32) for q in range(2)]
                    last = jnp.where(part_of[0], moved[0], jnp.where(part_of[1], moved[1], moved[2]))
                    parts.append(jnp.concatenate(pieces + [last], axis=0))
                for i in range(3):
                    high, low = split(jnp.where(lane96 < 96 - 32 * i, parts[i], parts[i + 1]))
                    lanes = pl.ds((group * 3 + i) * 128, 128)
                    b_high[column, target, lanes] = high
                    b_low[column, target, lanes] = low

    def product(column, left, depth=slice(None)):
        a_high, a_low = split(left)
        high, low = b_high[column, depth, :], b_low[column, depth, :]
        return jnp.dot(
            jnp.concatenate([a_high, a_high, a_low], axis=1),
            jnp.concatenate([high, low, high], axis=0),
            preferred_element_type=jnp.float32,
        )

    near = lax.div(x, 2)
    far = 1 - near
    same = pl.ds(pl.multiple_of(lax.rem(x, 2) * 384, 128), 384)
    other_block = pl.ds(pl.multiple_of((1 - lax.rem(x, 2)) * 384, 128), 384)

    def multiply(dz, core, half, whole=None, block=None, partly=None):
        zs = lax.rem(z + dz, 4)
        dy = lax.rem(zs + 4 - y, 4)
        first = (dy == 0) | ((dy == 3) & (half == 0)) | ((dy == 1) & (half == 1))
        rows = pl.ds(pl.multiple_of(half * 384, 384), 384)
        column = zs * 2 + core
        if whole is not None:

            @pl.when(whole(dy, first))
            def _():
                out_ref[rows, :] += product(column, amp[column, rows, :])

        if block is not None:

            @pl.when(partly(dy, first))
            def _():
                out_ref[rows, :] += product(column, amp[column, rows, block], block)

    def early(dy, first):
        return first

    def late(dy, first):
        return (dy != 2) & jnp.logical_not(first)

    own_flags.wait()
    locate(row)
    own_x.wait()
    pack()
    for block in blocks.values():
        block[PIECES:] = jnp.zeros((3, PIECE, 128), jnp.float32)
    out_ref[...] = jnp.zeros_like(out_ref)

    for half in halves:
        ring_send(half, 1, 0)
    for half in halves:
        ring_send(half, 2, 0)

    @pl.loop(0, 16)
    def _(source):
        locate(source)

    unpack(0, 0)
    for half in halves:
        ring_pass(half, 1, 0)
    for other in (3, 1):
        for half in halves:
            ring_send(half, 2, other)
    y_step(0)
    for half in halves:
        ring_pass(half, 2, 0)
    for key in ((0, 3), (0, 1), (3, 0), (1, 0)):
        unpack(*key)
    for half in halves:
        ring_last(half, 1, 0)
    for half in halves:
        ring_send(half, 2, 2)
    y_step(1)
    y_step(2)
    for half in halves:
        ring_pass(half, 2, 3)
    unpack(3, 3)
    for half in halves:
        ring_pass(half, 2, 1)
    for key in ((3, 1), (1, 3), (1, 1)):
        unpack(*key)
    y_step(3)
    own_amp.wait()
    shared["own"].wait_recv()
    for q in range(3):
        shared["below", q].wait_recv()
        shared["above", q + 3].wait_recv()

    @pl.loop(0, 6)
    def _(n):
        multiply(lax.rem(3 + lax.div(n, 2), 4), near, lax.rem(n, 2), early)

    for half in halves:
        ring_pass(half, 2, 2)
    y_step(4)

    @pl.loop(0, 6)
    def _(n):
        multiply(lax.rem(3 + lax.div(n, 2), 4), far, lax.rem(n, 2), None, other_block, early)

    for half in halves:
        ring_last(half, 2, 0)
    unpack(2, 0)
    unpack(0, 2)

    @pl.loop(0, 4)
    def _(n):
        entry = lax.div(n, 2)
        multiply(2 * entry, jnp.where(entry == 0, far, near), lax.rem(n, 2), None, same, early)

    y_step(5)
    for half in halves:
        ring_last(half, 2, 3)
    unpack(2, 3)
    unpack(3, 2)
    for q in range(3):
        shared["below", q + 3].wait_recv()
        shared["above", q].wait_recv()

    @pl.loop(0, 8)
    def _(n):
        entry = lax.div(n, 2)
        core = jnp.where(entry < 3, near, far)
        multiply(lax.rem(3 + entry, 4) * jnp.where(entry < 3, 1, 0), core, lax.rem(n, 2), late)

    @pl.loop(0, 2)
    def _(n):
        multiply(jnp.int32(3), far, n, late, same, early)

    for half in halves:
        ring_last(half, 2, 1)
    unpack(2, 1)
    unpack(1, 2)

    @pl.loop(0, 4)
    def _(n):
        entry = lax.div(n, 2)
        core = jnp.where(entry == 0, near, far)
        block = pl.ds(pl.multiple_of(jnp.where(entry == 0, other_block.start, same.start), 128), 384)
        multiply(2 - entry, core, lax.rem(n, 2), late, block, early)

    for half in halves:
        ring_last(half, 2, 2)
    unpack(2, 2)
    y_last(0)

    @pl.loop(0, 2)
    def _(n):
        multiply(jnp.int32(2), 1 - near, n, lambda dy, first: dy != 2)

    def finish(n, column):
        rows = [rows_of(q) for q in (up_order[n], down_order[n])]
        size = rows[0].size
        a_high, a_low = split(jnp.concatenate([amp[column, r, :] for r in rows], axis=0))
        value = jnp.dot(
            jnp.concatenate([a_high, a_low], axis=0), b_high[column], preferred_element_type=jnp.float32)
        value = value[: 2 * size] + value[2 * size :]
        value += jnp.dot(a_high, b_low[column], preferred_element_type=jnp.float32)
        out_ref[rows[0], :] += value[:size]
        out_ref[rows[1], :] += value[size:]

    def finish_shared(n):
        for q in (up_order[n], down_order[n]):
            shared["far", q].wait_recv()
        finish(n, column_of(2, 1 - k))

    finish(0, column_of(2, k))
    y_last(1)
    finish_shared(0)
    finish(1, column_of(2, k))
    y_last(2)
    finish_shared(1)
    finish(2, column_of(2, k))
    finish_shared(2)
    for copy in started:
        copy.wait_send()


COPIES = 2 * CHUNKS + 1 + CHUNKS + 3 * CHUNKS + 40


def body(amplitudes, integrals, flags):
    return pl.pallas_call(
        main_kernel,
        out_shape=pltpu.VMEM((768, 768), jnp.float32),
        in_specs=[
            pl.BlockSpec(memory_space=pl.ANY),
            pl.BlockSpec(memory_space=pl.ANY),
            pl.BlockSpec(memory_space=pl.ANY),
        ],
        out_specs=pl.BlockSpec(memory_space=pltpu.VMEM),
        scratch_shapes=[
            pltpu.VMEM((8, 768, 768), jnp.float32),
            pltpu.VMEM((8, 768, 768), jnp.bfloat16),
            pltpu.VMEM((8, 768, 768), jnp.bfloat16),
            pltpu.VMEM((768, 384), jnp.float32),
            pltpu.VMEM((384, 768), jnp.float32),
            pltpu.VMEM((96, PIECE, 128), jnp.float32),
            pltpu.SMEM((64, 64), jnp.int32),
            pltpu.SMEM((8, 64), jnp.int32),
        ]
        + [pltpu.VMEM((PIECES + 3, PIECE, 128), jnp.float32)] * 16
        + [
            pltpu.SemaphoreType.DMA((COPIES,)),
            pltpu.SemaphoreType.DMA((COPIES,)),
            pltpu.SemaphoreType.DMA((3,)),
        ],
        compiler_params=pltpu.CompilerParams(
            collective_id=0, has_side_effects=True, vmem_limit_bytes=62_000_000
        ),
        name="ladder",
    )(flags, amplitudes, integrals)


def solution(mesh):
    return jax.shard_map(
        body,
        mesh=mesh,
        in_specs=(P("row", "col"), P("col", "row"), P()),
        out_specs=P("row", "col"),
        check_vma=False,
    )
```
